32 devices in a mesh: seg: 4 (over y, core), sec: 8 (over z, x).
Axes of the slice: x: 2, y: 2, z: 4, core: 2. Of those that a mesh axis runs over, the one named last changes fastest.
Arguments:
- left_env: bfloat16 [4, 8, 3, 512, 512], P('seg', 'sec'), may hold values from -0.25 to 0.25
- right_env: bfloat16 [4, 8, 3, 512, 512], P('seg', 'sec'), may hold values from -0.25 to 0.25
- psi: bfloat16 [4, 8, 512, 512], P('seg', 'sec'), may hold values from -6 to 6
- orders: int32 [4, 8, 2], P('seg', 'sec'), may hold values from 64 to 512, as said below
- sources: int32 [3, 8], replicated, may hold values from 0 to 7, each once within a row
- active: int32 [4, 8, 3], P('seg', 'sec'), may hold values 0 or 1
Outputs:
- applied: bfloat16 [4, 8, 512, 512], P('seg', 'sec')
The draws below stay inside these ranges and needn't reach their ends.
Inputs may be any that keep to these rules, and one draw needn't show every extreme that they name: In every bond one sector has both orders equal to 512. `sources`: each row is a permutation of the sectors.
All inputs are finite; a program needn't handle non-finite values. No bound on the sum of `active` on one device may be relied on, other than what follows from the above.
Results may differ from the reference program's by a relative error of at most 0.008.
Values may be sent and summed in bfloat16 or wider, within the bound.
No kernel may reach another device: no remote copies, remote signals or barrier semaphores. Data moves between devices by JAX's collectives and lax.ppermute only.
A program may use at most 64 MiB of HBM per device.

```python
import jax
import jax.numpy as jnp
from jax import lax

B = 512
TERMS = 3
SECTORS = 8
BONDS = 4


def draw_orders(key, part):
    key_base, key_spot = jax.random.split(key)
    base = jax.random.randint(key_base, (BONDS, SECTORS, 2), B // 8, B + 1)
    spot = jax.random.randint(key_spot, (BONDS, 1, 1), 0, SECTORS)
    sector = lax.broadcasted_iota(jnp.int32, (BONDS, SECTORS, 2), 1)
    return jnp.where(sector == spot, B, base).astype(jnp.int32)


def touch_ends(entries, own_key, smallest, high):
    longest = entries.shape.index(max(entries.shape))
    spots = []
    for shift in (0, 1):
        where = [jax.random.randint(jax.random.fold_in(own_key, axis), (), 0, length) for axis, length in enumerate(entries.shape)]
        where[longest] = (where[longest] + shift) % entries.shape[longest]
        spots.append(tuple(where))
    return entries.at[spots[0]].set(smallest).at[spots[1]].set(high)


def levels(own_key, dims, shards, smallest, high):
    loudness, own = 1.0, jax.random.fold_in(own_key, 6)
    for position, shards_of in shards:
        heights = jnp.exp(jax.random.uniform(jax.random.fold_in(own, position), (shards_of,), jnp.float32, smallest / len(shards), high / len(shards)))
        loudness = loudness * jnp.repeat(heights, dims[position] // shards_of).reshape([-1 if axis == position else 1 for axis in range(len(dims))])
    return loudness


def bell_draw(rng, shape, spread, bound, shards=(), kind=jnp.bfloat16):
    level = levels(rng, shape, shards, -0.22, 0.18) if shards else 1.0
    values = jax.random.normal(rng, shape, jnp.float32) * spread * level
    return jnp.minimum(jnp.maximum(values, -bound), bound).astype(kind)


def setup_inputs(seed: int = 0) -> dict:
    arg_keys = jax.random.split(jax.random.key(seed), 7)
    return {
        "left_env": bell_draw(arg_keys[0], (BONDS, SECTORS, TERMS, B, B), B ** -0.5, 0.25, ((0, 4), (1, 8))),
        "right_env": bell_draw(arg_keys[1], (BONDS, SECTORS, TERMS, B, B), B ** -0.5, 0.25, ((0, 4), (1, 8))),
        "psi": bell_draw(arg_keys[2], (BONDS, SECTORS, B, B), 1.0, 6.0, ((0, 4), (1, 8))),
        "orders": draw_orders(jax.random.fold_in(arg_keys[6], 71), 0),
        "sources": jax.vmap(lambda own: jax.random.permutation(own, SECTORS))(jax.random.split(arg_keys[4], TERMS)).reshape((TERMS, SECTORS)).astype(jnp.int32),
        "active": touch_ends((jax.random.randint(arg_keys[5], (BONDS, SECTORS, TERMS), 0, 4) < 3).astype(jnp.int32), jax.random.fold_in(arg_keys[5], 1), 0, 1),
    }


def sector_masks(order_rows, padded):
    positions = jnp.arange(padded, dtype=jnp.int32)
    upper = positions[None, :, None] < order_rows[:, 0][:, None, None]
    lower = positions[None, None, :] < order_rows[:, 1][:, None, None]
    return upper & lower


def reference(left_env, right_env, psi, orders, sources, active):
    moved = jnp.roll(right_env, -1, axis=0)
    wanted = sources.T.astype(jnp.int32)

    def one_bond(packed):
        left_bond, right_bond, psi_bond, order_bond, active_bond = packed
        inside_mask = sector_masks(order_bond, psi_bond.shape[-1])
        masked_psi = jnp.where(inside_mask, psi_bond, jnp.zeros((), psi_bond.dtype))
        picked = masked_psi[wanted]
        left_product = jnp.einsum("swab,swbc->swac", left_bond.astype(jnp.float32), picked.astype(jnp.float32)).astype(jnp.bfloat16)
        full_product = jnp.einsum("swac,swdc->swad", left_product.astype(jnp.float32), right_bond.astype(jnp.float32))
        weights = active_bond.astype(jnp.float32)
        summed = jnp.sum(full_product * weights[:, :, None, None], axis=1)
        return jnp.where(inside_mask, summed, jnp.zeros((), summed.dtype)).astype(jnp.bfloat16)

    return lax.map(one_bond, (left_env, moved, psi, orders, active))
```

```python
import functools

import jax
import jax.numpy as jnp
from jax import lax
from jax.experimental import pallas as pl
from jax.experimental.pallas import tpu as pltpu
from jax.sharding import PartitionSpec as P

PAIR = 2


def place_in_ring(plane, planes):
    return jnp.where(plane % 2 == 1, (plane + 1) // 2, (planes - plane // 2) % planes)


def ring_route(planes):
    ring = [0, *range(1, planes, 2), *reversed(range(2, planes, 2))]
    steps = zip(ring, ring[1:] + ring[:1])
    return [(a * PAIR + c, b * PAIR + c) for a, b in steps for c in range(PAIR)]


def held_as(sector, holder, planes):
    at = place_in_ring(holder // PAIR, planes)
    of = place_in_ring(sector // PAIR, planes)
    return PAIR * lax.rem(at - of + planes, planes) + lax.rem(sector + holder, PAIR)


def slots_of(keys, last):
    slots = []
    for mine in keys:
        later = 0
        for i, other in enumerate(keys):
            fresh = (other > mine) & (other < last)
            for before in keys[:i]:
                fresh = fresh & (before != other)
            later = later + fresh.astype(jnp.int32)
        slots.append(len(keys) - 1 - later)
    return slots


def split_kernel(orders_ref, psi_ref, mine_ref, other_ref):
    rows, width = mine_ref.shape
    side = lax.rem(lax.axis_index("sec"), PAIR)
    row = lax.broadcasted_iota(jnp.int32, (rows, width), 0)
    column = lax.broadcasted_iota(jnp.int32, (rows, width), 1)
    for ref, half in ((mine_ref, side), (other_ref, PAIR - 1 - side)):
        start = pl.multiple_of(half * width, width)
        inside = (row < orders_ref[0, 0, 0]) & (column + start < orders_ref[0, 0, 1])
        values = psi_ref[0, 0, :, pl.ds(start, width)]
        ref[...] = jnp.where(inside, values, jnp.zeros((), values.dtype))


def choose_kernel(slot, planes, sources_ref, *refs):
    *held, out_ref, sem = refs
    terms = sources_ref.shape[0]
    me = lax.axis_index("sec")
    partner = me + 1 - PAIR * lax.rem(me, PAIR)
    last = PAIR * planes - 1
    keys = [held_as(sources_ref[w, partner], me, planes) for w in range(terms)]
    wanted = jnp.int32(0)
    for key, at in zip(keys, slots_of(keys, last)):
        wanted = jnp.where((at == slot) & (key < last), key, wanted)
    for i, ref in enumerate(held):

        @pl.when(wanted == i)
        def _(ref=ref):
            copy = pltpu.make_async_copy(ref, out_ref, sem)
            copy.start()
            copy.wait()


def apply_kernel(planes, sources_ref, active_ref, orders_ref, left_hbm, right_hbm, *refs):
    count = PAIR * planes
    held, refs = refs[:count], refs[count:]
    terms = sources_ref.shape[0]
    passed, refs = refs[: terms + 1], refs[terms + 1 :]
    out_ref, left, right, blocks, total, big_sem, block_sem = refs
    width = blocks.shape[-1]
    me = lax.axis_index("sec")
    side = lax.rem(me, PAIR)
    partner = me + 1 - PAIR * side
    last = count - 1
    wanted = [sources_ref[w, me] for w in range(terms)]
    keys = [held_as(s, partner, planes) for s in wanted]
    slots = slots_of(keys, last)
    for w in range(terms):
        pltpu.make_async_copy(left_hbm.at[0, 0, w], left.at[w], big_sem.at[0, w]).start()
        pltpu.make_async_copy(right_hbm.at[0, 0, w], right.at[w], big_sem.at[1, w]).start()
        own = held_as(wanted[w], me, planes)
        for i, ref in enumerate(held):

            @pl.when(own == i)
            def _(ref=ref):
                pltpu.make_async_copy(ref, blocks.at[w, 0], block_sem.at[w, 0]).start()

        for j, ref in enumerate(passed):

            @pl.when(jnp.where(keys[w] == last, terms, slots[w]) == j)
            def _(ref=ref):
                pltpu.make_async_copy(ref, blocks.at[w, 1], block_sem.at[w, 1]).start()

    total[...] = jnp.zeros_like(total)
    for w in range(terms):
        pltpu.make_async_copy(left_hbm.at[0, 0, w], left.at[w], big_sem.at[0, w]).wait()
        pltpu.make_async_copy(right_hbm.at[0, 0, w], right.at[w], big_sem.at[1, w]).wait()
        for h in range(PAIR):
            pltpu.make_async_copy(held[0], blocks.at[w, h], block_sem.at[w, h]).wait()

        @pl.when(active_ref[0, 0, w] != 0)
        def _():
            for h in range(PAIR):
                half = side if h == 0 else PAIR - 1 - side
                start = pl.multiple_of(half * width, width)
                product = jnp.dot(left[w], blocks[w, h], preferred_element_type=jnp.float32)
                total[...] += lax.dot_general(
                    product.astype(jnp.bfloat16),
                    right[w, :, pl.ds(start, width)],
                    (((1,), (1,)), ((), ())),
                    preferred_element_type=jnp.float32,
                )

    row = lax.broadcasted_iota(jnp.int32, total.shape, 0)
    column = lax.broadcasted_iota(jnp.int32, total.shape, 1)
    inside = (row < orders_ref[0, 0, 0]) & (column < orders_ref[0, 0, 1])
    out_ref[0, 0] = jnp.where(inside, total[...], 0.0).astype(out_ref.dtype)


SMEM = pl.BlockSpec(memory_space=pltpu.SMEM)
VMEM = pl.BlockSpec(memory_space=pltpu.VMEM)
ANY = pl.BlockSpec(memory_space=pl.ANY)


def body(left_env, right_env, psi, orders, sources, active):
    size = psi.shape[-1]
    terms = sources.shape[0]
    sectors = lax.axis_size("sec")
    planes = sectors // PAIR
    bonds = lax.axis_size("seg")
    half = jax.ShapeDtypeStruct((size, size // PAIR), psi.dtype)
    mine, other = pl.pallas_call(
        split_kernel, out_shape=(half, half), in_specs=[SMEM, VMEM], out_specs=(VMEM, VMEM), name="split"
    )(orders, psi)
    swap = [(i, i + 1 - PAIR * (i % PAIR)) for i in range(sectors)]
    ring = ring_route(planes)
    given = lax.ppermute(other, "sec", swap)
    held = [mine, given]
    shifted = lax.ppermute(right_env, "seg", [((i + 1) % bonds, i) for i in range(bonds)])
    passed = []
    while len(held) < sectors:
        held.append(lax.ppermute(held[-PAIR], "sec", ring))
        slot = len(held) - (sectors - 1) + terms - 1
        if 0 <= slot < terms:
            chosen = pl.pallas_call(
                functools.partial(choose_kernel, slot, planes),
                out_shape=half,
                in_specs=[SMEM] + [ANY] * len(held),
                out_specs=VMEM,
                scratch_shapes=[pltpu.SemaphoreType.DMA],
                name=f"choose_{slot}",
            )(sources, *held)
            passed.append(lax.ppermute(chosen, "sec", swap))
    passed.append(lax.ppermute(held[-1], "sec", swap))
    return pl.pallas_call(
        functools.partial(apply_kernel, planes),
        out_shape=jax.ShapeDtypeStruct(psi.shape, psi.dtype),
        in_specs=[SMEM] * 3 + [ANY] * (2 + len(held) + len(passed)),
        out_specs=VMEM,
        scratch_shapes=[
            pltpu.VMEM(left_env.shape[2:], left_env.dtype),
            pltpu.VMEM(right_env.shape[2:], right_env.dtype),
            pltpu.VMEM((terms, PAIR, size, size // PAIR), psi.dtype),
            pltpu.VMEM((size, size), jnp.float32),
            pltpu.SemaphoreType.DMA((2, terms)),
            pltpu.SemaphoreType.DMA((terms, PAIR)),
        ],
        name="apply",
    )(sources, active, orders, left_env, shifted, *held, *passed)


def solution(mesh):
    placed = (
        P("seg", "sec", None, None, None),
        P("seg", "sec", None, None, None),
        P("seg", "sec", None, None),
        P("seg", "sec", None),
        P(),
        P("seg", "sec", None),
    )
    return jax.shard_map(
        body, mesh=mesh, in_specs=placed, out_specs=P("seg", "sec", None, None), check_vma=False
    )
```

```python
import functools

import jax
import jax.numpy as jnp
from jax import lax
from jax.experimental import pallas as pl
from jax.experimental.pallas import tpu as pltpu
from jax.sharding import PartitionSpec as P


PAIR = 2


def place_in_ring(plane, planes):
    return jnp.where(plane % 2 == 1, (plane + 1) // 2, (planes - plane // 2) % planes)


def ring_route(planes):
    ring = [0, *range(1, planes, 2), *reversed(range(2, planes, 2))]
    steps = zip(ring, ring[1:] + ring[:1])
    return [(a * PAIR + c, b * PAIR + c) for a, b in steps for c in range(PAIR)]


def held_as(sector, holder, planes):
    at = place_in_ring(holder // PAIR, planes)
    of = place_in_ring(sector // PAIR, planes)
    return PAIR * lax.rem(at - of + planes, planes) + lax.rem(sector + holder, PAIR)


def slots_of(keys, last):
    slots = []
    for mine in keys:
        later = 0
        for i, other in enumerate(keys):
            fresh = (other > mine) & (other < last)
            for before in keys[:i]:
                fresh = fresh & (before != other)
            later = later + fresh.astype(jnp.int32)
        slots.append(jnp.where(mine == last, len(keys), len(keys) - 1 - later))
    return slots


class Plan:
    def __init__(self, terms):
        self.send, self.own, self.slot, self.active = 0, terms, 2 * terms, 3 * terms
        self.order = 4 * terms
        self.rows = 4 * terms + 2

    @staticmethod
    def read(ref, row):
        return jnp.max(ref[pl.ds(row, 1), :])


def fetch(pairs, sem):
    copies = [pltpu.make_async_copy(*pair, sem.at[i]) for i, pair in enumerate(pairs)]
    for copy in copies:
        copy.start()
    for copy in copies:
        copy.wait()


def plan_kernel(planes, sources_hbm, active_hbm, orders_hbm, out_ref, sources_ref, active_ref, orders_ref, sem):
    fetch([(sources_hbm, sources_ref), (active_hbm, active_ref), (orders_hbm, orders_ref)], sem)
    terms = sources_ref.shape[0]
    plan = Plan(terms)
    me = lax.axis_index("sec")
    partner = me + 1 - PAIR * lax.rem(me, PAIR)
    last = PAIR * planes - 1

    def put(row, value):
        out_ref[pl.ds(row, 1), :] = jnp.full((1, out_ref.shape[1]), value, jnp.int32)

    keys = [held_as(sources_ref[w, partner], me, planes) for w in range(terms)]
    slots = slots_of(keys, last)
    for slot in range(terms):
        wanted = jnp.int32(0)
        for key, at in zip(keys, slots):
            wanted = jnp.where(at == slot, key, wanted)
        put(plan.send + slot, wanted)
    wanted = [sources_ref[w, me] for w in range(terms)]
    slots = slots_of([held_as(s, partner, planes) for s in wanted], last)
    for w in range(terms):
        put(plan.own + w, held_as(wanted[w], me, planes))
        put(plan.slot + w, slots[w])
        put(plan.active + w, active_ref[0, 0, w])
    for side in range(2):
        put(plan.order + side, orders_ref[0, 0, side])


def split_kernel(orders_hbm, psi_hbm, mine_ref, other_ref, orders_ref, psi_ref, sem):
    fetch([(psi_hbm, psi_ref), (orders_hbm, orders_ref)], sem)
    rows, width = mine_ref.shape
    side = lax.rem(lax.axis_index("sec"), PAIR)
    row = lax.broadcasted_iota(jnp.int32, (rows, width), 0)
    column = lax.broadcasted_iota(jnp.int32, (rows, width), 1)
    for ref, half in ((other_ref, PAIR - 1 - side), (mine_ref, side)):
        start = pl.multiple_of(half * width, width)
        inside = (row < orders_ref[0, 0, 0]) & (column + start < orders_ref[0, 0, 1])
        values = psi_ref[0, 0, :, pl.ds(start, width)]
        ref[...] = jnp.where(inside, values, jnp.zeros((), values.dtype))


def choose_kernel(row, plan_ref, *refs):
    *held, out_ref = refs
    wanted = Plan.read(plan_ref, row)
    for i, ref in enumerate(held):

        @pl.when(wanted == i)
        def _(ref=ref):
            out_ref[...] = ref[...]


def apply_kernel(terms, owned, slotted, first, final, plan_ref, left_ref, right_ref, *refs):
    plan = Plan(terms)
    held, refs = refs[: len(owned)], refs[len(owned) :]
    passed, refs = refs[: len(slotted)], refs[len(slotted) :]
    if first:
        out_ref, blocks = refs
        total = out_ref
        total[...] = jnp.zeros_like(total)
    else:
        before_ref, out_ref, blocks, total = refs if final else (*refs, refs[1])
        total[...] = before_ref[...]
    width = blocks.shape[-1]
    side = lax.rem(lax.axis_index("sec"), PAIR)
    for w in range(terms):
        active = Plan.read(plan_ref, plan.active + w) != 0
        for kind, row, places, arrived in ((0, plan.own, owned, held), (1, plan.slot, slotted, passed)):
            if not places:
                continue
            at = Plan.read(plan_ref, row + w)
            for place, ref in zip(places, arrived):

                @pl.when(at == place)
                def _(ref=ref):
                    blocks[...] = ref[...]

            @pl.when(active & (at >= places[0]) & (at <= places[-1]))
            def _():
                half = side if kind == 0 else PAIR - 1 - side
                start = pl.multiple_of(half * width, width)
                product = jnp.dot(left_ref[0, 0, w], blocks[...], preferred_element_type=jnp.float32)
                total[...] += lax.dot_general(
                    product.astype(blocks.dtype),
                    right_ref[0, 0, w, :, pl.ds(start, width)],
                    (((1,), (1,)), ((), ())),
                    preferred_element_type=jnp.float32,
                )

    if final:
        row = lax.broadcasted_iota(jnp.int32, total.shape, 0)
        column = lax.broadcasted_iota(jnp.int32, total.shape, 1)
        inside = (row < Plan.read(plan_ref, plan.order)) & (column < Plan.read(plan_ref, plan.order + 1))
        out_ref[0, 0] = jnp.where(inside, total[...], 0.0).astype(out_ref.dtype)


ROOM = pltpu.CompilerParams(vmem_limit_bytes=24 << 20)
HBM = pl.BlockSpec(memory_space=pltpu.HBM)
VMEM = pl.BlockSpec(memory_space=pltpu.VMEM)


def near(array):
    return pltpu.with_memory_space_constraint(array, pltpu.VMEM)


def far(array):
    return pltpu.with_memory_space_constraint(array, pltpu.HBM)


def body(left_env, right_env, psi, orders, sources, active):
    size = psi.shape[-1]
    terms = sources.shape[0]
    sectors = lax.axis_size("sec")
    planes = sectors // PAIR
    bonds = lax.axis_size("seg")
    half = pltpu.VMEM((size, size // PAIR), psi.dtype)
    sums = pltpu.VMEM((size, size), jnp.float32)
    swap = [(i, i + 1 - PAIR * (i % PAIR)) for i in range(sectors)]
    ring = ring_route(planes)

    def kernel(fn, operands, **kwargs):
        return pl.pallas_call(fn, compiler_params=ROOM, **kwargs)(*operands)

    mine, other = kernel(
        split_kernel,
        (far(orders), far(psi)),
        out_shape=(half, half),
        in_specs=[HBM] * 2,
        out_specs=(VMEM, VMEM),
        scratch_shapes=[
            pltpu.SMEM(orders.shape, orders.dtype),
            pltpu.VMEM(psi.shape, psi.dtype),
            pltpu.SemaphoreType.DMA((2,)),
        ],
    )
    plan = kernel(
        functools.partial(plan_kernel, planes),
        (far(sources), far(active), far(orders)),
        out_shape=pltpu.VMEM((Plan(terms).rows, 128), jnp.int32),
        in_specs=[HBM] * 3,
        out_specs=VMEM,
        scratch_shapes=[pltpu.SMEM(x.shape, x.dtype) for x in (sources, active, orders)]
        + [pltpu.SemaphoreType.DMA((3,))],
    )
    held = [mine, lax.ppermute(other, "sec", swap)]
    left = near(left_env)
    right = near(lax.ppermute(right_env, "seg", [((i + 1) % bonds, i) for i in range(bonds)]))
    while len(held) < sectors:
        held.append(lax.ppermute(held[-PAIR], "sec", ring))
    passed = []
    for slot in range(terms):
        usable = held[: sectors - terms + slot]
        chosen = kernel(
            functools.partial(choose_kernel, Plan(terms).send + slot),
            [near(x) for x in (plan, *usable)],
            out_shape=half,
            in_specs=[VMEM] * (1 + len(usable)),
            out_specs=VMEM,
        )
        passed.append(lax.ppermute(chosen, "sec", swap))
    passed.append(lax.ppermute(held[-1], "sec", swap))

    stages = (
        (range(sectors - 2), range(0)),
        (range(sectors - 2, sectors - 1), range(terms - 2)),
        (range(sectors - 1, sectors), range(terms - 2, terms)),
        (range(0), range(terms, terms + 1)),
    )
    total = []
    for i, (owned, slotted) in enumerate(stages):
        final = i == len(stages) - 1
        operands = [plan, left, right, *(held[j] for j in owned), *(passed[j] for j in slotted), *total]
        total = [
            kernel(
                functools.partial(apply_kernel, terms, owned, slotted, i == 0, final),
                [near(x) for x in operands],
                out_shape=jax.ShapeDtypeStruct(psi.shape, psi.dtype) if final else sums,
                in_specs=[VMEM] * len(operands),
                out_specs=VMEM,
                scratch_shapes=[half] + [sums] * final,
            )
        ]
    return total[0]


def solution(mesh):
    placed = (
        P("seg", "sec", None, None, None),
        P("seg", "sec", None, None, None),
        P("seg", "sec", None, None),
        P("seg", "sec", None),
        P(),
        P("seg", "sec", None),
    )

    def program(*args):
        step = jax.shard_map(body, mesh=mesh, in_specs=placed, out_specs=P("seg", "sec", None, None), check_vma=False)
        return step(*args)

    return program
```
